256 devices in a mesh: gx: 16 (over y_lo, z), gz: 16 (over y_hi, x, core).
Axes of the slice: x: 4, y: 4 (y_hi: 2, y_lo: 2; y = y_hi * 2 + y_lo), z: 8, core: 2. Of those that a mesh axis runs over, the one named last changes fastest.
Arguments:
- temp: float32 [256, 1024, 256], P('gz', 'gx'), may hold values from -6 to 6
- u_vel: float32 [256, 1024, 256], P('gz', 'gx'), may hold values from -1.8 to 1.8
- v_vel: float32 [256, 1024, 256], P('gz', 'gx'), may hold values from -1.8 to 1.8
- w_vel: float32 [256, 1024, 256], P('gz', 'gx'), may hold values from -1.8 to 1.8
- temp_prev_tend: float32 [256, 1024, 256], P('gz', 'gx'), may hold values from -6 to 6
- w_prev_tend: float32 [256, 1024, 256], P('gz', 'gx'), may hold values from -6 to 6
- lower_coupling: float32 [256], P('gz'), may hold values from 256 to 4096
- upper_coupling: float32 [256], P('gz'), may hold values from 256 to 4096, as said below
- vertical_metric: float32 [256], P('gz'), may hold values from 0.25 to 2
Outputs:
- temp_next: float32 [256, 1024, 256], P('gz', 'gx')
- w_next: float32 [256, 1024, 256], P('gz', 'gx')
- temp_tend: float32 [256, 1024, 256], P('gz', 'gx')
- w_tend: float32 [256, 1024, 256], P('gz', 'gx')
The draws below stay inside these ranges and needn't reach their ends.
Inputs may be any that keep to these rules, and one draw needn't show every extreme that they name: upper_coupling[k] equals lower_coupling[k + 1] for k < 255: the face shared by two levels.
All inputs are finite; a program needn't handle non-finite values.
Results may differ from the reference program's by a relative error of at most 0.0003.
Values sent between devices are 32-bit elements; how exact they have to be, the bound alone decides.
A program may use at most 128 MiB of HBM per device.

```python
import math
import jax
import jax.numpy as jnp
from jax import lax

CZ = 16
NY = 256
NZ = 256
NX = 1024


def coupling_faces(key):
    spread = jax.random.uniform(jax.random.fold_in(key, 11), (NZ + 1,), jnp.float32)
    return CZ * CZ * jnp.exp(spread * math.log(16.0))


def draw_lower_coupling(key, part):
    return coupling_faces(key)[:NZ]


def draw_upper_coupling(key, part):
    return coupling_faces(key)[1:]


def draw_temp(key, part):
    noise_key = jax.random.fold_in(key, 5)
    return jnp.clip(jax.random.normal(noise_key, (NZ, NX, NY), jnp.float32), -6.0, 6.0)


def block_scale(stream_key, dims, pieces, low, largest):
    loudness, own = 1.0, jax.random.fold_in(stream_key, 6)
    for axis_at, parts in pieces:
        draws = jnp.exp(jax.random.uniform(jax.random.fold_in(own, axis_at), (parts,), jnp.float32, low / len(pieces), largest / len(pieces)))
        loudness = loudness * jnp.repeat(draws, dims[axis_at] // parts).reshape([-1 if axis == axis_at else 1 for axis in range(len(dims))])
    return loudness


def gaussian(key, dims, deviation, most, split=(), held_as=jnp.bfloat16):
    entries = deviation * jax.random.normal(key, dims, jnp.float32)
    if split:
        entries = entries * block_scale(key, dims, split, -0.22, 0.18)
    return jnp.clip(entries, -most, most).astype(held_as)


def setup_inputs(seed: int = 0) -> dict:
    arg_keys = jax.random.split(jax.random.key(seed), 10)
    return {
        "temp": draw_temp(jax.random.fold_in(arg_keys[9], 71), 0),
        "u_vel": gaussian(arg_keys[1], (NZ, NX, NY), 0.3, 1.8, ((0, 16), (1, 16)), jnp.float32),
        "v_vel": gaussian(arg_keys[2], (NZ, NX, NY), 0.3, 1.8, ((0, 16), (1, 16)), jnp.float32),
        "w_vel": gaussian(arg_keys[3], (NZ, NX, NY), 0.3, 1.8, ((0, 16), (1, 16)), jnp.float32),
        "temp_prev_tend": gaussian(arg_keys[4], (NZ, NX, NY), 1.0, 6.0, ((0, 16), (1, 16)), jnp.float32),
        "w_prev_tend": gaussian(arg_keys[5], (NZ, NX, NY), 1.0, 6.0, ((0, 16), (1, 16)), jnp.float32),
        "lower_coupling": draw_lower_coupling(jax.random.fold_in(arg_keys[9], 71), 0),
        "upper_coupling": draw_upper_coupling(jax.random.fold_in(arg_keys[9], 71), 0),
        "vertical_metric": jnp.clip(jnp.exp(math.log(2.0) - 2.0794415 * jax.random.uniform(arg_keys[8], (NZ,), jnp.float32) ** block_scale(arg_keys[8], (NZ,), ((0, 16),), -0.2, 0.2)), 0.25, 2.0),
    }


NEW_WEIGHT = 5.0 / 12.0
OLD_WEIGHT = -17.0 / 60.0
HORIZ_DIFF = 0.1


def tendency(field, u_vel, v_vel, w_vel, vertical_metric, source):
    flux_x = u_vel * field
    advect = 0.5 * (jnp.roll(flux_x, -1, 1) - jnp.roll(flux_x, 1, 1))
    flux_y = v_vel * field
    advect = advect + 0.5 * (jnp.roll(flux_y, -1, 2) - jnp.roll(flux_y, 1, 2))
    flux_z = jnp.pad(w_vel * field, ((1, 1), (0, 0), (0, 0)))
    advect = advect + vertical_metric[:, None, None] * (flux_z[2:] - flux_z[:-2])
    spread = jnp.roll(field, -1, 1) + jnp.roll(field, 1, 1) + jnp.roll(field, -1, 2) + jnp.roll(field, 1, 2) - 4.0 * field
    return -advect + HORIZ_DIFF * spread + source


def vertical_diffusion(field, lower_coupling, upper_coupling):
    padded = jnp.pad(field, ((1, 1), (0, 0), (0, 0)))
    return upper_coupling[:, None, None] * (padded[2:] - field) - lower_coupling[:, None, None] * (field - padded[:-2])


def sweep_solve(low_band, main_band, high_band, right_side):
    def forward(carry, row):
        ratio_prev, value_prev = carry
        low_val, main_val, high_val, rhs_row = row
        pivot_val = main_val - low_val * ratio_prev
        ratio_new = high_val / pivot_val
        value_new = (rhs_row - low_val * value_prev) / pivot_val
        return (ratio_new, value_new), (ratio_new, value_new)

    start = (jnp.zeros((), jnp.float32), jnp.zeros(right_side.shape[1:], jnp.float32))
    _, (ratios, values) = lax.scan(forward, start, (low_band, main_band, high_band, right_side))

    def backward(next_value, row):
        ratio_row, value_row = row
        solved_row = value_row - ratio_row * next_value
        return solved_row, solved_row

    _, solved = lax.scan(backward, jnp.zeros(right_side.shape[1:], jnp.float32), (ratios, values), reverse=True)
    return solved


def reference(temp, u_vel, v_vel, w_vel, temp_prev_tend, w_prev_tend, lower_coupling, upper_coupling, vertical_metric):
    temp_tend = tendency(temp, u_vel, v_vel, w_vel, vertical_metric, w_vel)
    w_tend = tendency(w_vel, u_vel, v_vel, w_vel, vertical_metric, temp)
    low_band = -lower_coupling
    main_band = 1.0 + lower_coupling + upper_coupling
    high_band = -upper_coupling
    temp_rhs = temp + vertical_diffusion(temp, lower_coupling, upper_coupling) + NEW_WEIGHT * temp_tend + OLD_WEIGHT * temp_prev_tend
    temp_next = sweep_solve(low_band, main_band, high_band, temp_rhs)
    w_rhs = w_vel + vertical_diffusion(w_vel, lower_coupling, upper_coupling) + NEW_WEIGHT * w_tend + OLD_WEIGHT * w_prev_tend
    w_next = sweep_solve(low_band, main_band, high_band, w_rhs)
    return (temp_next, w_next, temp_tend, w_tend)
```

```python
import functools

import jax
import jax.numpy as jnp
from jax import lax
from jax.experimental import pallas as pl
from jax.experimental.pallas import tpu as pltpu
from jax.sharding import PartitionSpec as P

NEW_WEIGHT = 5.0 / 12.0
OLD_WEIGHT = -17.0 / 60.0
HORIZ_DIFF = 0.1
MESH = pl.DeviceIdType.MESH
PAD = 8


def exchange_kernel(
    n, temp, u_vel, v_vel, w_vel, temp_old, w_old, lower, upper, metric,
    part_t, part_w, tend_t, tend_w, state, basis,
    tbuf, ubuf, wbuf, vbuf, tobuf, wobuf,
    low_s, up_s, met_s,
    inv, mine, mats, edge_out, edge_lo, edge_hi, below, above,
    ends, gathered, sols, entry,
    load_sem, scal_sem, mat_send, mat_recv, edge_send, edge_recv, wall_send, wall_recv,
    fwd_send, fwd_recv, back_send, back_recv,
):
    levels, rows, cols = temp.shape
    halves = cols // 128
    blocks = rows // 8
    me = lax.axis_index("gz")
    gx = lax.axis_index("gx")
    nx = lax.axis_size("gx")
    right = lax.rem(gx + 1, nx)
    left = lax.rem(gx + nx - 1, nx)

    scal = [
        pltpu.make_async_copy(src, dst, scal_sem.at[i])
        for i, (src, dst) in enumerate(((lower, low_s), (upper, up_s), (metric, met_s)))
    ]
    for c in scal:
        c.start()
    loads = []
    for i, (src, dst) in enumerate(
        ((temp, tbuf), (w_vel, wbuf), (u_vel, ubuf), (v_vel, vbuf), (temp_old, tobuf), (w_old, wobuf))
    ):
        first = PAD if i < 3 else 0
        for h in range(halves):
            c = pltpu.make_async_copy(
                src.at[:, :, pl.ds(h * 128, 128)],
                dst.at[:, h, pl.ds(first, rows), :],
                load_sem.at[i, h],
            )
            c.start()
            loads.append(c)

    barrier = pltpu.get_barrier_semaphore()
    for step in range(1, n):
        pl.semaphore_signal(
            barrier, inc=1, device_id={"gz": lax.rem(me + step, n)}, device_id_type=MESH
        )
    for other in (left, right):
        pl.semaphore_signal(barrier, inc=1, device_id={"gx": other}, device_id_type=MESH)

    for c in scal:
        c.wait()
    one = jnp.ones((8, 128), jnp.float32)
    zero = jnp.zeros((8, 128), jnp.float32)
    phi, phi_flux, psi, psi_flux = one, zero, zero, one
    for k in range(levels):
        inv_k = 1.0 / (one * up_s[k])
        inv[k] = inv_k
        basis[0, k] = phi
        basis[1, k] = psi
        phi_flux = phi_flux + phi
        psi_flux = psi_flux + psi
        phi = phi + phi_flux * inv_k
        psi = psi + psi_flux * inv_k
    sub = lax.broadcasted_iota(jnp.int32, (8, 128), 0)
    mine[0] = phi
    mine[1] = psi
    mine[2] = phi_flux
    mine[3] = psi_flux
    mat = jnp.where(sub == 0, phi, zero)
    mat = jnp.where(sub == 1, psi, mat)
    mat = jnp.where(sub == 2, phi_flux, mat)
    mat = jnp.where(sub == 3, psi_flux, mat)
    mat = jnp.where(sub == 4, one * low_s[0], mat)
    mats[me] = mat

    pl.semaphore_wait(barrier, n + 1)

    up_copies = [
        pltpu.make_async_remote_copy(
            src_ref=src.at[levels - 1],
            dst_ref=below.at[i],
            send_sem=wall_send.at[0, i],
            recv_sem=wall_recv.at[0, i],
            device_id={"gz": lax.rem(me + 1, n)},
            device_id_type=MESH,
        )
        for i, src in enumerate((temp, w_vel))
    ]
    down_copies = [
        pltpu.make_async_remote_copy(
            src_ref=src.at[0],
            dst_ref=above.at[i],
            send_sem=wall_send.at[1, i],
            recv_sem=wall_recv.at[1, i],
            device_id={"gz": lax.rem(me + n - 1, n)},
            device_id_type=MESH,
        )
        for i, src in enumerate((temp, w_vel))
    ]

    @pl.when(me < n - 1)
    def _():
        for c in up_copies:
            c.start()

    @pl.when(me > 0)
    def _():
        for c in down_copies:
            c.start()

    @pl.when(me == 0)
    def _():
        below[...] = jnp.zeros_like(below)

    @pl.when(me == n - 1)
    def _():
        above[...] = jnp.zeros_like(above)

    def mat_copy(step):
        return pltpu.make_async_remote_copy(
            src_ref=mats.at[me],
            dst_ref=mats.at[me],
            send_sem=mat_send.at[step],
            recv_sem=mat_recv.at[step],
            device_id={"gz": lax.rem(me + step, n)},
            device_id_type=MESH,
        )

    for step in range(1, n):
        mat_copy(step).start()

    for c in loads[: 3 * halves]:
        c.wait()
    for k in range(levels):
        for a, buf in enumerate((tbuf, wbuf, ubuf)):
            for h in range(halves):
                edge_out[0, a, h, pl.ds(k, 1), :] = buf[k, h, pl.ds(PAD, 1), :]
                edge_out[1, a, h, pl.ds(k, 1), :] = buf[k, h, pl.ds(PAD + rows - 1, 1), :]
    to_left = pltpu.make_async_remote_copy(
        src_ref=edge_out.at[0], dst_ref=edge_hi, send_sem=edge_send.at[0], recv_sem=edge_recv.at[0],
        device_id={"gx": left}, device_id_type=MESH,
    )
    to_right = pltpu.make_async_remote_copy(
        src_ref=edge_out.at[1], dst_ref=edge_lo, send_sem=edge_send.at[1], recv_sem=edge_recv.at[1],
        device_id={"gx": right}, device_id_type=MESH,
    )
    to_left.start()
    to_right.start()
    for c in loads[3 * halves :]:
        c.wait()

    lane = lax.broadcasted_iota(jnp.int32, (8, 128), 1)
    first_lane = lane == 0
    last_lane = lane == 127

    def next_col(g):
        r = [pltpu.roll(x, 127, 1) for x in g]
        return [jnp.where(last_lane, r[(h + 1) % halves], r[h]) for h in range(halves)]

    def prev_col(g):
        r = [pltpu.roll(x, 1, 1) for x in g]
        return [jnp.where(first_lane, r[(h - 1) % halves], r[h]) for h in range(halves)]

    def block(step, carry):
        ib = jnp.where(step < blocks - 2, step + 1, jnp.where(step == blocks - 2, 0, blocks - 1))

        @pl.when(step == blocks - 2)
        def _():
            to_left.wait_recv()
            to_right.wait_recv()
            for k in range(levels):
                for a, buf in enumerate((tbuf, wbuf, ubuf)):
                    for h in range(halves):
                        buf[k, h, pl.ds(PAD - 1, 1), :] = edge_lo[a, h, pl.ds(k, 1), :]
                        buf[k, h, pl.ds(PAD + rows, 1), :] = edge_hi[a, h, pl.ds(k, 1), :]

        row = pl.multiple_of(ib * 8, 8)
        H = range(halves)

        def center(buf, k):
            return [buf[k, h, pl.ds(row + PAD, 8), :] for h in H]

        y = [[zero for _ in H] for _ in range(2)]
        flux = [[zero for _ in H] for _ in range(2)]
        f = [center(tbuf, 0), center(wbuf, 0)]
        wf = [[f[1][h] * f[q][h] for h in H] for q in range(2)]
        wf_below = [[zero for _ in H] for _ in range(2)]
        for k in range(levels):
            if k < levels - 1:
                f_up = [center(tbuf, k + 1), center(wbuf, k + 1)]
                wf_up = [[f_up[1][h] * f_up[q][h] for h in H] for q in range(2)]
            else:
                f_up, wf_up = None, [[zero for _ in H] for _ in range(2)]
            m_k = met_s[k]
            inv_k = inv[k]
            from_hi, from_lo, y_hi, y_lo = [], [], [], []
            for h in H:
                from_hi.append(HORIZ_DIFF - 0.5 * ubuf[k, h, pl.ds(row + PAD + 1, 8), :])
                from_lo.append(HORIZ_DIFF + 0.5 * ubuf[k, h, pl.ds(row + PAD - 1, 8), :])
                hv = 0.5 * vbuf[k, h, pl.ds(row, 8), :]
                y_hi.append(HORIZ_DIFF - hv)
                y_lo.append(HORIZ_DIFF + hv)
            for q, (buf, old, tend, part) in enumerate(
                ((tbuf, tobuf, tend_t, part_t), (wbuf, wobuf, tend_w, part_w))
            ):
                nxt = next_col([f[q][h] * y_hi[h] for h in H])
                prv = prev_col([f[q][h] * y_lo[h] for h in H])
                for h in H:
                    acc = (
                        buf[k, h, pl.ds(row + PAD + 1, 8), :] * from_hi[h]
                        + buf[k, h, pl.ds(row + PAD - 1, 8), :] * from_lo[h]
                    )
                    acc = acc + (nxt[h] + prv[h])
                    acc = acc + (f[1 - q][h] - (4.0 * HORIZ_DIFF) * f[q][h])
                    acc = acc + m_k * (wf_below[q][h] - wf_up[q][h])
                    tend[k, pl.ds(row, 8), pl.ds(h * 128, 128)] = acc
                    rhs = (
                        (f[q][h] + f[q][h])
                        + NEW_WEIGHT * acc
                        + OLD_WEIGHT * old[k, h, pl.ds(row, 8), :]
                    )
                    part[k, pl.ds(row, 8), pl.ds(h * 128, 128)] = y[q][h] - f[q][h]
                    flux[q][h] = flux[q][h] + (y[q][h] - rhs)
                    y[q][h] = y[q][h] + flux[q][h] * inv_k
            wf_below, wf, f = wf, wf_up, f_up
        for h in H:
            for q in range(2):
                ends[ib * halves + h, 2 * q] = y[q][h]
                ends[ib * halves + h, 2 * q + 1] = flux[q][h]
        return carry

    lax.fori_loop(0, blocks, block, 0)

    @pl.when(me > 0)
    def _():
        for c in up_copies:
            c.wait_recv()

    @pl.when(me < n - 1)
    def _():
        for c in down_copies:
            c.wait_recv()

    m_lo = NEW_WEIGHT * met_s[0]
    m_hi = NEW_WEIGHT * met_s[levels - 1]

    def fwd_copy(step):
        to = lax.rem(me + step, n)
        return pltpu.make_async_remote_copy(
            src_ref=ends.at[to],
            dst_ref=gathered.at[me],
            send_sem=fwd_send.at[step],
            recv_sem=fwd_recv.at[step],
            device_id={"gz": to},
            device_id_type=MESH,
        )

    def tile_of(buf, tile, q):
        r = pl.multiple_of((tile // halves) * 8, 8)
        c = pl.multiple_of(lax.rem(tile, halves) * 128, 128)
        return buf[q, pl.ds(r, 8), pl.ds(c, 128)]

    def fix(tile):
        for q in range(2):
            lo = m_lo * (tile_of(below, tile, 1) * tile_of(below, tile, q))
            hi = m_hi * (tile_of(above, tile, 1) * tile_of(above, tile, q))
            ends[tile, 2 * q] = ends[tile, 2 * q] - mine[1] * lo + inv[levels - 1] * hi
            ends[tile, 2 * q + 1] = ends[tile, 2 * q + 1] - mine[3] * lo + hi

    for step in range(1, n):
        fix(lax.rem(me + step, n))
        fwd_copy(step).start()
    fix(me)
    gathered[me] = ends[me]

    for q, tend in enumerate((tend_t, tend_w)):
        tend[0] = tend[0] + met_s[0] * (below[1] * below[q])
        tend[levels - 1] = tend[levels - 1] - met_s[levels - 1] * (above[1] * above[q])

    for step in range(1, n):
        mat_copy(step).wait_recv()

    def entry_of(d, r):
        return jnp.broadcast_to(mats[d, pl.ds(r, 1), :], (8, 128))

    bottom = [(one, entry_of(0, 4))]
    for d in range(n):
        a, b = bottom[-1]
        bottom.append(
            (entry_of(d, 0) * a + entry_of(d, 1) * b, entry_of(d, 2) * a + entry_of(d, 3) * b)
        )
    top = [(zero, one)]
    for d in range(n - 1, -1, -1):
        a, b = top[-1]
        top.append(
            (entry_of(d, 3) * a + entry_of(d, 1) * b, entry_of(d, 2) * a + entry_of(d, 0) * b)
        )
    top = top[::-1]
    scale = 1.0 / bottom[n][0]

    for step in range(1, n):
        fwd_copy(step).wait_recv()

    for q in range(2):
        amp = [None] * n
        run = zero
        for d in range(n - 1, -1, -1):
            a, b = top[d + 1]
            run = run - (gathered[d, 2 * q] * b + gathered[d, 2 * q + 1] * a)
            amp[d] = run * scale
        run = zero
        for d in range(n):
            bot, up = bottom[d], top[d]
            beta = run * scale
            sols[d, 2 * q] = bot[0] * amp[d] - up[0] * beta
            sols[d, 2 * q + 1] = bot[1] * amp[d] + up[1] * beta
            a, b = bottom[d + 1]
            run = run + (a * gathered[d, 2 * q + 1] - b * gathered[d, 2 * q])

    def back_copy(step):
        to = lax.rem(me + step, n)
        return pltpu.make_async_remote_copy(
            src_ref=sols.at[to],
            dst_ref=entry.at[me],
            send_sem=back_send.at[step],
            recv_sem=back_recv.at[step],
            device_id={"gz": to},
            device_id_type=MESH,
        )

    for step in range(1, n):
        back_copy(step).start()
    entry[me] = sols[me]
    for step in range(1, n):
        back_copy(step).wait_recv()
    for tile in range(n):
        r, c = 8 * (tile // halves), 128 * (tile % halves)
        for q in range(2):
            lo = m_lo * (
                below[1, pl.ds(r, 8), pl.ds(c, 128)] * below[q, pl.ds(r, 8), pl.ds(c, 128)]
            )
            state[2 * q, pl.ds(r, 8), pl.ds(c, 128)] = entry[tile, 2 * q]
            state[2 * q + 1, pl.ds(r, 8), pl.ds(c, 128)] = entry[tile, 2 * q + 1] - lo

    @pl.when(me < n - 1)
    def _():
        for c in up_copies:
            c.wait_send()

    @pl.when(me > 0)
    def _():
        for c in down_copies:
            c.wait_send()

    to_left.wait_send()
    to_right.wait_send()
    for step in range(1, n):
        mat_copy(step).wait_send()
        fwd_copy(step).wait_send()
        back_copy(step).wait_send()


def finish_kernel(
    part_t, part_w, tend_t, tend_w, state, basis,
    temp_next, w_next, tend_t_out, tend_w_out,
    xbuf, sems,
):
    levels, rows, cols = part_t.shape
    outs = [
        pltpu.make_async_copy(tend_t, tend_t_out, sems.at[0]),
        pltpu.make_async_copy(tend_w, tend_w_out, sems.at[1]),
    ]
    for c in outs:
        c.start()

    def level(k):
        phi = jnp.concatenate([basis[0, k]] * (cols // 128), axis=1)[:1]
        psi = jnp.concatenate([basis[1, k]] * (cols // 128), axis=1)[:1]
        for q, part in enumerate((part_t, part_w)):
            xbuf[q, k] = part[k] + phi * state[2 * q] + psi * state[2 * q + 1]

    for k in range(levels):
        level(k)
        for q, out in enumerate((temp_next, w_next)):
            c = pltpu.make_async_copy(xbuf.at[q, k], out.at[k], sems.at[2 + q * levels + k])
            c.start()
            outs.append(c)
    for c in outs:
        c.wait()


def local(n, temp, u_vel, v_vel, w_vel, temp_old, w_old, lower, upper, metric):
    levels, rows, cols = temp.shape
    halves = cols // 128
    f32 = jnp.float32
    cube = jax.ShapeDtypeStruct((levels, rows, cols), f32)
    hbm = pl.BlockSpec(memory_space=pltpu.HBM)
    vmem = pl.BlockSpec(memory_space=pltpu.VMEM)
    dma = pltpu.SemaphoreType.DMA
    padded = pltpu.VMEM((levels, halves, rows + 2 * PAD, 128), f32)
    plain = pltpu.VMEM((levels, halves, rows, 128), f32)
    edge = (3, halves, levels, 128)
    parts = pl.pallas_call(
        functools.partial(exchange_kernel, n),
        out_shape=(
            cube, cube, cube, cube,
            jax.ShapeDtypeStruct((4, rows, cols), f32),
            jax.ShapeDtypeStruct((2, levels, 8, 128), f32),
        ),
        in_specs=[hbm] * 9,
        out_specs=(vmem,) * 6,
        scratch_shapes=[
            padded, padded, padded, plain, plain, plain,
            pltpu.SMEM((levels,), f32), pltpu.SMEM((levels,), f32), pltpu.SMEM((levels,), f32),
            pltpu.VMEM((levels, 8, 128), f32),
            pltpu.VMEM((4, 8, 128), f32),
            pltpu.VMEM((n, 8, 128), f32),
            pltpu.VMEM((2, *edge), f32),
            pltpu.VMEM(edge, f32),
            pltpu.VMEM(edge, f32),
            pltpu.VMEM((2, rows, cols), f32),
            pltpu.VMEM((2, rows, cols), f32),
            pltpu.VMEM((n, 4, 8, 128), f32),
            pltpu.VMEM((n, 4, 8, 128), f32),
            pltpu.VMEM((n, 4, 8, 128), f32),
            pltpu.VMEM((n, 4, 8, 128), f32),
            dma((6, halves)), dma((3,)),
            dma((n,)), dma((n,)), dma((2,)), dma((2,)), dma((2, 2)), dma((2, 2)),
            dma((n,)), dma((n,)), dma((n,)), dma((n,)),
        ],
        compiler_params=pltpu.CompilerParams(
            collective_id=0, has_side_effects=True, vmem_limit_bytes=40 * 1024 * 1024
        ),
        name="exchange",
    )(
        *(
            pltpu.with_memory_space_constraint(x, pltpu.HBM)
            for x in (temp, u_vel, v_vel, w_vel, temp_old, w_old, lower, upper, metric)
        )
    )
    return pl.pallas_call(
        finish_kernel,
        out_shape=(cube,) * 4,
        in_specs=[vmem] * 6,
        out_specs=(hbm,) * 4,
        scratch_shapes=[pltpu.VMEM((2, levels, rows, cols), f32), dma((2 + 2 * levels,))],
        compiler_params=pltpu.CompilerParams(vmem_limit_bytes=24 * 1024 * 1024),
        name="finish",
    )(*parts)


def solution(mesh):
    cube = P("gz", "gx", None)
    line = P("gz")
    return jax.shard_map(
        functools.partial(local, mesh.shape["gz"]),
        mesh=mesh,
        in_specs=(cube,) * 6 + (line,) * 3,
        out_specs=(cube,) * 4,
        check_vma=False,
    )
```

```python
import functools

import jax
import jax.numpy as jnp
from jax import lax
from jax.experimental import pallas as pl
from jax.experimental.pallas import tpu as pltpu
from jax.sharding import PartitionSpec as P

NEW_WEIGHT = 5.0 / 12.0
OLD_WEIGHT = -17.0 / 60.0
HORIZ_DIFF = 0.1
MESH = pl.DeviceIdType.MESH
PAD = 8


def exchange_kernel(
    n, temp, u_vel, v_vel, w_vel, temp_old, w_old, lower, upper, metric,
    part_t, part_w, tend_t, tend_w, state, basis,
    tbuf, ubuf, wbuf, vbuf, tobuf, wobuf,
    low_s, up_s, met_s,
    inv, mine, mats, edge_out, edge_lo, edge_hi, below, above,
    ends, gathered, sols, entry,
    load_sem, scal_sem, mat_send, mat_recv, edge_send, edge_recv, wall_send, wall_recv,
    fwd_send, fwd_recv, back_send, back_recv,
):
    levels, rows, cols = temp.shape
    halves = cols // 128
    blocks = rows // 8
    me = lax.axis_index("gz")
    gx = lax.axis_index("gx")
    nx = lax.axis_size("gx")
    right = lax.rem(gx + 1, nx)
    left = lax.rem(gx + nx - 1, nx)

    scal = [
        pltpu.make_async_copy(src, dst, scal_sem.at[i])
        for i, (src, dst) in enumerate(((lower, low_s), (upper, up_s), (metric, met_s)))
    ]
    for c in scal:
        c.start()
    loads = []
    for i, (src, dst) in enumerate(
        ((temp, tbuf), (w_vel, wbuf), (u_vel, ubuf), (v_vel, vbuf), (temp_old, tobuf), (w_old, wobuf))
    ):
        first = PAD if i < 3 else 0
        for h in range(halves):
            c = pltpu.make_async_copy(
                src.at[:, :, pl.ds(h * 128, 128)],
                dst.at[:, h, pl.ds(first, rows), :],
                load_sem.at[i, h],
            )
            c.start()
            loads.append(c)

    barrier = pltpu.get_barrier_semaphore()
    for step in range(1, n):
        pl.semaphore_signal(
            barrier, inc=1, device_id={"gz": lax.rem(me + step, n)}, device_id_type=MESH
        )
    for other in (left, right):
        pl.semaphore_signal(barrier, inc=1, device_id={"gx": other}, device_id_type=MESH)

    for c in scal:
        c.wait()
    one = jnp.ones((8, 128), jnp.float32)
    zero = jnp.zeros((8, 128), jnp.float32)
    phi, phi_flux, psi, psi_flux = one, zero, zero, one
    for k in range(levels):
        inv_k = 1.0 / (one * up_s[k])
        inv[k] = inv_k
        basis[0, k] = phi
        basis[1, k] = psi
        phi_flux = phi_flux + phi
        psi_flux = psi_flux + psi
        phi = phi + phi_flux * inv_k
        psi = psi + psi_flux * inv_k
    sub = lax.broadcasted_iota(jnp.int32, (8, 128), 0)
    mine[0] = phi
    mine[1] = psi
    mine[2] = phi_flux
    mine[3] = psi_flux
    mat = jnp.where(sub == 0, phi, zero)
    mat = jnp.where(sub == 1, psi, mat)
    mat = jnp.where(sub == 2, phi_flux, mat)
    mat = jnp.where(sub == 3, psi_flux, mat)
    mat = jnp.where(sub == 4, one * low_s[0], mat)
    mat = jnp.where(sub == 5, one * met_s[0], mat)
    mat = jnp.where(sub == 6, one * met_s[levels - 1], mat)
    mats[me] = mat

    pl.semaphore_wait(barrier, n + 1)

    def mat_copy(step):
        return pltpu.make_async_remote_copy(
            src_ref=mats.at[me],
            dst_ref=mats.at[me],
            send_sem=mat_send.at[step],
            recv_sem=mat_recv.at[step],
            device_id={"gz": lax.rem(me + step, n)},
            device_id_type=MESH,
        )

    for step in (1, n - 1, *range(2, n - 1)):
        mat_copy(step).start()

    up_copies = [
        pltpu.make_async_remote_copy(
            src_ref=src.at[levels - 1],
            dst_ref=below.at[i],
            send_sem=wall_send.at[0, i],
            recv_sem=wall_recv.at[0, i],
            device_id={"gz": lax.rem(me + 1, n)},
            device_id_type=MESH,
        )
        for i, src in enumerate((temp, w_vel))
    ]
    down_copies = [
        pltpu.make_async_remote_copy(
            src_ref=src.at[0],
            dst_ref=above.at[i],
            send_sem=wall_send.at[1, i],
            recv_sem=wall_recv.at[1, i],
            device_id={"gz": lax.rem(me + n - 1, n)},
            device_id_type=MESH,
        )
        for i, src in enumerate((temp, w_vel))
    ]

    @pl.when(me < n - 1)
    def _():
        for c in up_copies:
            c.start()

    @pl.when(me > 0)
    def _():
        for c in down_copies:
            c.start()

    @pl.when(me == 0)
    def _():
        below[...] = jnp.zeros_like(below)

    @pl.when(me == n - 1)
    def _():
        above[...] = jnp.zeros_like(above)

    for c in loads[: 3 * halves]:
        c.wait()
    for k in range(levels):
        for a, buf in enumerate((tbuf, wbuf, ubuf)):
            for h in range(halves):
                edge_out[0, a, h, pl.ds(k, 1), :] = buf[k, h, pl.ds(PAD, 1), :]
                edge_out[1, a, h, pl.ds(k, 1), :] = buf[k, h, pl.ds(PAD + rows - 1, 1), :]
    to_left = pltpu.make_async_remote_copy(
        src_ref=edge_out.at[0], dst_ref=edge_hi, send_sem=edge_send.at[0], recv_sem=edge_recv.at[0],
        device_id={"gx": left}, device_id_type=MESH,
    )
    to_right = pltpu.make_async_remote_copy(
        src_ref=edge_out.at[1], dst_ref=edge_lo, send_sem=edge_send.at[1], recv_sem=edge_recv.at[1],
        device_id={"gx": right}, device_id_type=MESH,
    )
    to_left.start()
    to_right.start()
    for c in loads[3 * halves :]:
        c.wait()

    lane = lax.broadcasted_iota(jnp.int32, (8, 128), 1)
    first_lane = lane == 0
    last_lane = lane == 127

    def next_col(g):
        r = [pltpu.roll(x, 127, 1) for x in g]
        return [jnp.where(last_lane, r[(h + 1) % halves], r[h]) for h in range(halves)]

    def prev_col(g):
        r = [pltpu.roll(x, 1, 1) for x in g]
        return [jnp.where(first_lane, r[(h - 1) % halves], r[h]) for h in range(halves)]

    def block(ib):
        row = pl.multiple_of(ib * 8, 8)
        H = range(halves)

        def center(buf, k):
            return [buf[k, h, pl.ds(row + PAD, 8), :] for h in H]

        y = [[zero for _ in H] for _ in range(2)]
        flux = [[zero for _ in H] for _ in range(2)]
        f = [center(tbuf, 0), center(wbuf, 0)]
        wf = [[f[1][h] * f[q][h] for h in H] for q in range(2)]
        wf_below = [[zero for _ in H] for _ in range(2)]
        for k in range(levels):
            if k < levels - 1:
                f_up = [center(tbuf, k + 1), center(wbuf, k + 1)]
                wf_up = [[f_up[1][h] * f_up[q][h] for h in H] for q in range(2)]
            else:
                f_up, wf_up = None, [[zero for _ in H] for _ in range(2)]
            m_k = met_s[k]
            inv_k = inv[k]
            from_hi, from_lo, y_hi, y_lo = [], [], [], []
            for h in H:
                from_hi.append(HORIZ_DIFF - 0.5 * ubuf[k, h, pl.ds(row + PAD + 1, 8), :])
                from_lo.append(HORIZ_DIFF + 0.5 * ubuf[k, h, pl.ds(row + PAD - 1, 8), :])
                hv = 0.5 * vbuf[k, h, pl.ds(row, 8), :]
                y_hi.append(HORIZ_DIFF - hv)
                y_lo.append(HORIZ_DIFF + hv)
            for q, (buf, old, tend, part) in enumerate(
                ((tbuf, tobuf, tend_t, part_t), (wbuf, wobuf, tend_w, part_w))
            ):
                nxt = next_col([f[q][h] * y_hi[h] for h in H])
                prv = prev_col([f[q][h] * y_lo[h] for h in H])
                for h in H:
                    acc = (
                        buf[k, h, pl.ds(row + PAD + 1, 8), :] * from_hi[h]
                        + buf[k, h, pl.ds(row + PAD - 1, 8), :] * from_lo[h]
                    )
                    acc = acc + (nxt[h] + prv[h])
                    acc = acc + (f[1 - q][h] - (4.0 * HORIZ_DIFF) * f[q][h])
                    acc = acc + m_k * (wf_below[q][h] - wf_up[q][h])
                    tend[k, pl.ds(row, 8), pl.ds(h * 128, 128)] = acc
                    rhs = (
                        (f[q][h] + f[q][h])
                        + NEW_WEIGHT * acc
                        + OLD_WEIGHT * old[k, h, pl.ds(row, 8), :]
                    )
                    part[k, pl.ds(row, 8), pl.ds(h * 128, 128)] = y[q][h] - f[q][h]
                    flux[q][h] = flux[q][h] + (y[q][h] - rhs)
                    y[q][h] = y[q][h] + flux[q][h] * inv_k
            wf_below, wf, f = wf, wf_up, f_up
        for h in H:
            for q in range(2):
                ends[ib * halves + h, 2 * q] = y[q][h]
                ends[ib * halves + h, 2 * q + 1] = flux[q][h]

    def fwd_copy(tile, src, dst):
        return pltpu.make_async_remote_copy(
            src_ref=ends.at[tile],
            dst_ref=gathered.at[src],
            send_sem=fwd_send.at[dst],
            recv_sem=fwd_recv.at[src],
            device_id={"gz": dst},
            device_id_type=MESH,
        )

    stride = 5

    def fix_and_send(tile):
        ib = tile // halves
        h = lax.rem(tile, halves)
        r = pl.multiple_of(ib * 8 + PAD, 8)
        for q, buf in enumerate((tbuf, wbuf)):
            lo = m_below * (wbuf[0, h, pl.ds(r, 8), :] * buf[0, h, pl.ds(r, 8), :])
            hi = m_above * (wbuf[levels - 1, h, pl.ds(r, 8), :] * buf[levels - 1, h, pl.ds(r, 8), :])
            ends[tile, 2 * q] = ends[tile, 2 * q] + low_value * lo
            ends[tile, 2 * q + 1] = ends[tile, 2 * q + 1] + low_flux * lo - hi
        dst = lax.rem(tile * stride, n)

        @pl.when(dst != me)
        def _():
            fwd_copy(tile, me, dst).start()

        @pl.when(dst == me)
        def _():
            gathered[me] = ends[tile]

    inner = blocks - 2

    def inner_step(s, carry):
        block(s + 1)
        return carry

    lax.fori_loop(0, inner, inner_step, 0)

    above_id = lax.rem(me + 1, n)
    below_id = lax.rem(me + n - 1, n)
    mat_copy(1).wait_recv()
    mat_copy(n - 1).wait_recv()
    m_above = jnp.where(me < n - 1, NEW_WEIGHT, 0.0) * jnp.broadcast_to(
        mats[above_id, pl.ds(5, 1), :], (8, 128)
    )
    m_below = jnp.where(me > 0, NEW_WEIGHT, 0.0) * jnp.broadcast_to(
        mats[below_id, pl.ds(6, 1), :], (8, 128)
    )
    inv_low = 1.0 / (one * low_s[0])
    low_value = mine[0] * inv_low + mine[1]
    low_flux = mine[2] * inv_low + mine[3]

    def inner_send(s, carry):
        fix_and_send(halves + lax.rem(me + s, inner * halves))
        return carry

    lax.fori_loop(0, inner * halves, inner_send, 0)

    to_left.wait_recv()
    to_right.wait_recv()
    for k in range(levels):
        for a, buf in enumerate((tbuf, wbuf, ubuf)):
            for h in range(halves):
                buf[k, h, pl.ds(PAD - 1, 1), :] = edge_lo[a, h, pl.ds(k, 1), :]
                buf[k, h, pl.ds(PAD + rows, 1), :] = edge_hi[a, h, pl.ds(k, 1), :]

    def outer_step(s, carry):
        block(s * (blocks - 1))
        return carry

    lax.fori_loop(0, 2, outer_step, 0)

    def outer_send(s, carry):
        t = lax.rem(me + s, 2 * halves)
        fix_and_send(jnp.where(t < halves, t, t + inner * halves))
        return carry

    lax.fori_loop(0, 2 * halves, outer_send, 0)

    @pl.when(me > 0)
    def _():
        for c in up_copies:
            c.wait_recv()

    @pl.when(me < n - 1)
    def _():
        for c in down_copies:
            c.wait_recv()

    for q, tend in enumerate((tend_t, tend_w)):
        tend[0] = tend[0] + met_s[0] * (below[1] * below[q])
        tend[levels - 1] = tend[levels - 1] - met_s[levels - 1] * (above[1] * above[q])

    for step in range(2, n - 1):
        mat_copy(step).wait_recv()

    def entry_of(d, r):
        return jnp.broadcast_to(mats[d, pl.ds(r, 1), :], (8, 128))

    bottom = [(one, entry_of(0, 4))]
    for d in range(n):
        a, b = bottom[-1]
        bottom.append(
            (entry_of(d, 0) * a + entry_of(d, 1) * b, entry_of(d, 2) * a + entry_of(d, 3) * b)
        )
    top = [(zero, one)]
    for d in range(n - 1, -1, -1):
        a, b = top[-1]
        top.append(
            (entry_of(d, 3) * a + entry_of(d, 1) * b, entry_of(d, 2) * a + entry_of(d, 0) * b)
        )
    top = top[::-1]
    scale = 1.0 / bottom[n][0]

    for step in range(1, n):
        fwd_copy(0, lax.rem(me + step, n), me).wait_recv()

    for q in range(2):
        amp = [None] * n
        run = zero
        for d in range(n - 1, -1, -1):
            a, b = top[d + 1]
            run = run - (gathered[d, 2 * q] * b + gathered[d, 2 * q + 1] * a)
            amp[d] = run * scale
        run = zero
        for d in range(n):
            bot, up = bottom[d], top[d]
            beta = run * scale
            sols[d, 2 * q] = bot[0] * amp[d] - up[0] * beta
            sols[d, 2 * q + 1] = bot[1] * amp[d] + up[1] * beta
            a, b = bottom[d + 1]
            run = run + (a * gathered[d, 2 * q + 1] - b * gathered[d, 2 * q])

    def back_copy(step):
        to = lax.rem(me + step, n)
        return pltpu.make_async_remote_copy(
            src_ref=sols.at[to],
            dst_ref=entry.at[me],
            send_sem=back_send.at[step],
            recv_sem=back_recv.at[step],
            device_id={"gz": to},
            device_id_type=MESH,
        )

    for step in range(1, n):
        back_copy(step).start()
    entry[me] = sols[me]
    for step in range(1, n):
        back_copy(step).wait_recv()
    for tile in range(n):
        ib, h = tile // halves, tile % halves
        r, c = 8 * ib, 128 * h
        own = (tile * stride) % n
        for q, buf in enumerate((tbuf, wbuf)):
            lo = m_below * (wbuf[0, h, pl.ds(r + PAD, 8), :] * buf[0, h, pl.ds(r + PAD, 8), :])
            state[2 * q, pl.ds(r, 8), pl.ds(c, 128)] = entry[own, 2 * q] + inv_low * lo
            state[2 * q + 1, pl.ds(r, 8), pl.ds(c, 128)] = entry[own, 2 * q + 1] + lo

    @pl.when(me < n - 1)
    def _():
        for c in up_copies:
            c.wait_send()

    @pl.when(me > 0)
    def _():
        for c in down_copies:
            c.wait_send()

    to_left.wait_send()
    to_right.wait_send()
    for step in range(1, n):
        mat_copy(step).wait_send()
        fwd_copy(0, me, lax.rem(me + step, n)).wait_send()
        back_copy(step).wait_send()


def finish_kernel(
    part_t, part_w, tend_t, tend_w, state, basis,
    temp_next, w_next, tend_t_out, tend_w_out,
    xbuf, sems,
):
    levels, rows, cols = part_t.shape
    outs = [
        pltpu.make_async_copy(tend_t, tend_t_out, sems.at[0]),
        pltpu.make_async_copy(tend_w, tend_w_out, sems.at[1]),
    ]
    for c in outs:
        c.start()

    def level(k):
        phi = jnp.concatenate([basis[0, k]] * (cols // 128), axis=1)[:1]
        psi = jnp.concatenate([basis[1, k]] * (cols // 128), axis=1)[:1]
        for q, part in enumerate((part_t, part_w)):
            xbuf[q, k] = part[k] + phi * state[2 * q] + psi * state[2 * q + 1]

    for k in range(levels):
        level(k)
        for q, out in enumerate((temp_next, w_next)):
            c = pltpu.make_async_copy(xbuf.at[q, k], out.at[k], sems.at[2 + q * levels + k])
            c.start()
            outs.append(c)
    for c in outs:
        c.wait()


def local(n, temp, u_vel, v_vel, w_vel, temp_old, w_old, lower, upper, metric):
    levels, rows, cols = temp.shape
    halves = cols // 128
    f32 = jnp.float32
    cube = jax.ShapeDtypeStruct((levels, rows, cols), f32)
    hbm = pl.BlockSpec(memory_space=pltpu.HBM)
    vmem = pl.BlockSpec(memory_space=pltpu.VMEM)
    dma = pltpu.SemaphoreType.DMA
    padded = pltpu.VMEM((levels, halves, rows + 2 * PAD, 128), f32)
    plain = pltpu.VMEM((levels, halves, rows, 128), f32)
    edge = (3, halves, levels, 128)
    parts = pl.pallas_call(
        functools.partial(exchange_kernel, n),
        out_shape=(
            cube, cube, cube, cube,
            jax.ShapeDtypeStruct((4, rows, cols), f32),
            jax.ShapeDtypeStruct((2, levels, 8, 128), f32),
        ),
        in_specs=[hbm] * 9,
        out_specs=(vmem,) * 6,
        scratch_shapes=[
            padded, padded, padded, plain, plain, plain,
            pltpu.SMEM((levels,), f32), pltpu.SMEM((levels,), f32), pltpu.SMEM((levels,), f32),
            pltpu.VMEM((levels, 8, 128), f32),
            pltpu.VMEM((4, 8, 128), f32),
            pltpu.VMEM((n, 8, 128), f32),
            pltpu.VMEM((2, *edge), f32),
            pltpu.VMEM(edge, f32),
            pltpu.VMEM(edge, f32),
            pltpu.VMEM((2, rows, cols), f32),
            pltpu.VMEM((2, rows, cols), f32),
            pltpu.VMEM((n, 4, 8, 128), f32),
            pltpu.VMEM((n, 4, 8, 128), f32),
            pltpu.VMEM((n, 4, 8, 128), f32),
            pltpu.VMEM((n, 4, 8, 128), f32),
            dma((6, halves)), dma((3,)),
            dma((n,)), dma((n,)), dma((2,)), dma((2,)), dma((2, 2)), dma((2, 2)),
            dma((n,)), dma((n,)), dma((n,)), dma((n,)),
        ],
        compiler_params=pltpu.CompilerParams(
            collective_id=0, has_side_effects=True, vmem_limit_bytes=40 * 1024 * 1024
        ),
        name="exchange",
    )(
        *(
            pltpu.with_memory_space_constraint(x, pltpu.HBM)
            for x in (temp, u_vel, v_vel, w_vel, temp_old, w_old, lower, upper, metric)
        )
    )
    return pl.pallas_call(
        finish_kernel,
        out_shape=(cube,) * 4,
        in_specs=[vmem] * 6,
        out_specs=(hbm,) * 4,
        scratch_shapes=[pltpu.VMEM((2, levels, rows, cols), f32), dma((2 + 2 * levels,))],
        compiler_params=pltpu.CompilerParams(vmem_limit_bytes=24 * 1024 * 1024),
        name="finish",
    )(*parts)


def solution(mesh):
    cube = P("gz", "gx", None)
    line = P("gz")
    return jax.shard_map(
        functools.partial(local, mesh.shape["gz"]),
        mesh=mesh,
        in_specs=(cube,) * 6 + (line,) * 3,
        out_specs=(cube,) * 4,
        check_vma=False,
    )
```

```python
import functools

import jax
import jax.numpy as jnp
from jax import lax
from jax.experimental import pallas as pl
from jax.experimental.pallas import tpu as pltpu
from jax.sharding import PartitionSpec as P

NEW_WEIGHT = 5.0 / 12.0
OLD_WEIGHT = -17.0 / 60.0
HORIZ_DIFF = 0.1
MESH = pl.DeviceIdType.MESH
PAD = 8


def hops(mask):
    along_x = (0, 1, 2, 1)[(mask >> 1) & 3]
    return 4 * (along_x + 2 * (mask >> 3)) + (mask & 1)


def far_first(n):
    return sorted(range(1, n), key=hops, reverse=True)


def exchange_kernel(
    n, temp, u_vel, v_vel, w_vel, temp_old, w_old, lower, upper, metric,
    part_t, part_w, tend_t, tend_w, state, basis,
    tbuf, ubuf, wbuf, vbuf, tobuf, wobuf,
    low_s, up_s, met_s,
    inv, mine, mats, edge_out, edge_in, edge_part, below, above,
    ends, gathered, sols, entry,
    load_sem, scal_sem, mat_send, mat_recv, edge_send, edge_recv, wall_send, wall_recv,
    fwd_send, fwd_recv, back_send, back_recv,
):
    levels, rows, cols = temp.shape
    halves = cols // 128
    blocks = rows // 8
    me = lax.axis_index("gz")
    gx = lax.axis_index("gx")
    nx = lax.axis_size("gx")
    right = lax.rem(gx + 1, nx)
    left = lax.rem(gx + nx - 1, nx)

    scal = [
        pltpu.make_async_copy(src, dst, scal_sem.at[i])
        for i, (src, dst) in enumerate(((lower, low_s), (upper, up_s), (metric, met_s)))
    ]
    for c in scal:
        c.start()
    loads = []
    for i, (src, dst) in enumerate(
        ((temp, tbuf), (w_vel, wbuf), (u_vel, ubuf), (v_vel, vbuf), (temp_old, tobuf), (w_old, wobuf))
    ):
        first = PAD if i < 3 else 0
        for h in range(halves):
            c = pltpu.make_async_copy(
                src.at[:, :, pl.ds(h * 128, 128)],
                dst.at[:, h, pl.ds(first, rows), :],
                load_sem.at[i, h],
            )
            c.start()
            loads.append(c)

    def clear(k, carry):
        for buf in (tbuf, wbuf, ubuf):
            for h in range(halves):
                buf[k, h, pl.ds(0, PAD), :] = jnp.zeros((PAD, 128), jnp.float32)
                buf[k, h, pl.ds(rows + PAD, PAD), :] = jnp.zeros((PAD, 128), jnp.float32)
        return carry

    barrier = pltpu.get_barrier_semaphore()
    for other in (left, right):
        pl.semaphore_signal(barrier, inc=1, device_id={"gx": other}, device_id_type=MESH)
    for mask in far_first(n):
        pl.semaphore_signal(
            barrier, inc=1, device_id={"gz": jnp.bitwise_xor(me, mask)}, device_id_type=MESH
        )

    lax.fori_loop(0, levels, clear, 0)
    for c in loads[: 3 * halves]:
        c.wait()

    def pack(k, carry):
        for e, (row, sign) in enumerate(((PAD, -0.5), (PAD + rows - 1, 0.5))):
            for h in range(halves):
                weight = HORIZ_DIFF + sign * ubuf[k, h, pl.ds(row, 1), :]
                for q, buf in enumerate((tbuf, wbuf)):
                    edge_out[e, k, pl.ds(q * halves + h, 1), :] = weight * buf[k, h, pl.ds(row, 1), :]
        return carry

    lax.fori_loop(0, levels, pack, 0)

    for c in scal:
        c.wait()
    one = jnp.ones((8, 128), jnp.float32)
    zero = jnp.zeros((8, 128), jnp.float32)
    phi, phi_flux, psi, psi_flux = one, zero, zero, one
    for k in range(levels):
        inv_k = 1.0 / (one * up_s[k])
        inv[k] = inv_k
        basis[0, k] = phi
        basis[1, k] = psi
        phi_flux = phi_flux + phi
        psi_flux = psi_flux + psi
        phi = phi + phi_flux * inv_k
        psi = psi + psi_flux * inv_k
    sub = lax.broadcasted_iota(jnp.int32, (8, 128), 0)
    mine[0] = phi
    mine[1] = psi
    mine[2] = phi_flux
    mine[3] = psi_flux
    mat = jnp.where(sub == 0, phi, zero)
    mat = jnp.where(sub == 1, psi, mat)
    mat = jnp.where(sub == 2, phi_flux, mat)
    mat = jnp.where(sub == 3, psi_flux, mat)
    mat = jnp.where(sub == 4, one * low_s[0], mat)
    mat = jnp.where(sub == 5, one * met_s[0], mat)
    mat = jnp.where(sub == 6, one * met_s[levels - 1], mat)
    mats[me] = mat

    pl.semaphore_wait(barrier, n + 1)

    to_left = pltpu.make_async_remote_copy(
        src_ref=edge_out.at[0], dst_ref=edge_in.at[1], send_sem=edge_send.at[0], recv_sem=edge_recv.at[0],
        device_id={"gx": left}, device_id_type=MESH,
    )
    to_right = pltpu.make_async_remote_copy(
        src_ref=edge_out.at[1], dst_ref=edge_in.at[0], send_sem=edge_send.at[1], recv_sem=edge_recv.at[1],
        device_id={"gx": right}, device_id_type=MESH,
    )
    to_left.start()
    to_right.start()

    def mat_copy(src, dst):
        return pltpu.make_async_remote_copy(
            src_ref=mats.at[me],
            dst_ref=mats.at[src],
            send_sem=mat_send.at[dst],
            recv_sem=mat_recv.at[src],
            device_id={"gz": dst},
            device_id_type=MESH,
        )

    above_id = lax.rem(me + 1, n)
    below_id = lax.rem(me + n - 1, n)
    mat_copy(me, above_id).start()
    mat_copy(me, below_id).start()
    for mask in far_first(n):
        dst = jnp.bitwise_xor(me, mask)

        @pl.when(jnp.logical_and(dst != above_id, dst != below_id))
        def _():
            mat_copy(me, dst).start()

    up_copies = [
        pltpu.make_async_remote_copy(
            src_ref=src.at[levels - 1],
            dst_ref=below.at[i],
            send_sem=wall_send.at[0, i],
            recv_sem=wall_recv.at[0, i],
            device_id={"gz": lax.rem(me + 1, n)},
            device_id_type=MESH,
        )
        for i, src in enumerate((temp, w_vel))
    ]
    down_copies = [
        pltpu.make_async_remote_copy(
            src_ref=src.at[0],
            dst_ref=above.at[i],
            send_sem=wall_send.at[1, i],
            recv_sem=wall_recv.at[1, i],
            device_id={"gz": lax.rem(me + n - 1, n)},
            device_id_type=MESH,
        )
        for i, src in enumerate((temp, w_vel))
    ]

    @pl.when(me == 0)
    def _():
        below[...] = jnp.zeros_like(below)

    @pl.when(me == n - 1)
    def _():
        above[...] = jnp.zeros_like(above)

    for c in loads[3 * halves :]:
        c.wait()

    lane = lax.broadcasted_iota(jnp.int32, (8, 128), 1)
    first_lane = lane == 0
    last_lane = lane == 127

    def next_col(g):
        r = [pltpu.roll(x, 127, 1) for x in g]
        return [jnp.where(last_lane, r[(h + 1) % halves], r[h]) for h in range(halves)]

    def prev_col(g):
        r = [pltpu.roll(x, 1, 1) for x in g]
        return [jnp.where(first_lane, r[(h - 1) % halves], r[h]) for h in range(halves)]

    def block(ib):
        row = pl.multiple_of(ib * 8, 8)
        H = range(halves)

        def center(buf, k):
            return [buf[k, h, pl.ds(row + PAD, 8), :] for h in H]

        y = [[zero for _ in H] for _ in range(2)]
        flux = [[zero for _ in H] for _ in range(2)]
        f = [center(tbuf, 0), center(wbuf, 0)]
        wf = [[f[1][h] * f[q][h] for h in H] for q in range(2)]
        wf_below = [[zero for _ in H] for _ in range(2)]
        for k in range(levels):
            if k < levels - 1:
                f_up = [center(tbuf, k + 1), center(wbuf, k + 1)]
                wf_up = [[f_up[1][h] * f_up[q][h] for h in H] for q in range(2)]
            else:
                f_up, wf_up = None, [[zero for _ in H] for _ in range(2)]
            m_k = met_s[k]
            inv_k = inv[k]
            from_hi, from_lo, y_hi, y_lo = [], [], [], []
            for h in H:
                from_hi.append(HORIZ_DIFF - 0.5 * ubuf[k, h, pl.ds(row + PAD + 1, 8), :])
                from_lo.append(HORIZ_DIFF + 0.5 * ubuf[k, h, pl.ds(row + PAD - 1, 8), :])
                hv = 0.5 * vbuf[k, h, pl.ds(row, 8), :]
                y_hi.append(HORIZ_DIFF - hv)
                y_lo.append(HORIZ_DIFF + hv)
            for q, (buf, old, tend, part) in enumerate(
                ((tbuf, tobuf, tend_t, part_t), (wbuf, wobuf, tend_w, part_w))
            ):
                nxt = next_col([f[q][h] * y_hi[h] for h in H])
                prv = prev_col([f[q][h] * y_lo[h] for h in H])
                for h in H:
                    acc = (
                        buf[k, h, pl.ds(row + PAD + 1, 8), :] * from_hi[h]
                        + buf[k, h, pl.ds(row + PAD - 1, 8), :] * from_lo[h]
                    )
                    acc = acc + (nxt[h] + prv[h])
                    acc = acc + (f[1 - q][h] - (4.0 * HORIZ_DIFF) * f[q][h])
                    acc = acc + m_k * (wf_below[q][h] - wf_up[q][h])
                    tend[k, pl.ds(row, 8), pl.ds(h * 128, 128)] = acc
                    rhs = (
                        (f[q][h] + f[q][h])
                        + NEW_WEIGHT * acc
                        + OLD_WEIGHT * old[k, h, pl.ds(row, 8), :]
                    )
                    part[k, pl.ds(row, 8), pl.ds(h * 128, 128)] = y[q][h] - f[q][h]
                    flux[q][h] = flux[q][h] + (y[q][h] - rhs)
                    y[q][h] = y[q][h] + flux[q][h] * inv_k
            wf_below, wf, f = wf, wf_up, f_up
        for h in H:
            for q in range(2):
                ends[ib * halves + h, 2 * q] = y[q][h]
                ends[ib * halves + h, 2 * q + 1] = flux[q][h]

    def fwd_copy(tile, src, dst):
        return pltpu.make_async_remote_copy(
            src_ref=ends.at[tile],
            dst_ref=gathered.at[src],
            send_sem=fwd_send.at[dst],
            recv_sem=fwd_recv.at[src],
            device_id={"gz": dst},
            device_id_type=MESH,
        )

    stride = 5

    back_stride = pow(stride, -1, n)

    def fix(tile):
        ib = tile // halves
        h = lax.rem(tile, halves)
        r = pl.multiple_of(ib * 8 + PAD, 8)
        for q, buf in enumerate((tbuf, wbuf)):
            lo = m_below * (wbuf[0, h, pl.ds(r, 8), :] * buf[0, h, pl.ds(r, 8), :])
            hi = m_above * (wbuf[levels - 1, h, pl.ds(r, 8), :] * buf[levels - 1, h, pl.ds(r, 8), :])
            ends[tile, 2 * q] = ends[tile, 2 * q] + low_value * lo
            ends[tile, 2 * q + 1] = ends[tile, 2 * q + 1] + low_flux * lo - hi

    def send(inner_tiles):
        for mask in far_first(n):
            dst = jnp.bitwise_xor(me, mask)
            tile = lax.rem(dst * back_stride, n)
            inside = jnp.logical_and(tile >= halves, tile < n - halves)

            @pl.when(inside if inner_tiles else jnp.logical_not(inside))
            def _():
                fwd_copy(tile, me, dst).start()

    inner = blocks - 2

    def block_step(ib, carry):
        block(ib)
        return carry

    lax.fori_loop(0, blocks, block_step, 0)

    mat_copy(above_id, me).wait_recv()
    mat_copy(below_id, me).wait_recv()
    m_above = jnp.where(me < n - 1, NEW_WEIGHT, 0.0) * jnp.broadcast_to(
        mats[above_id, pl.ds(5, 1), :], (8, 128)
    )
    m_below = jnp.where(me > 0, NEW_WEIGHT, 0.0) * jnp.broadcast_to(
        mats[below_id, pl.ds(6, 1), :], (8, 128)
    )
    inv_low = 1.0 / (one * low_s[0])
    low_value = mine[0] * inv_low + mine[1]
    low_flux = mine[2] * inv_low + mine[3]

    def fix_step(tile, carry):
        fix(tile)
        return carry

    lax.fori_loop(0, n, fix_step, 0)
    send(True)

    to_left.wait_recv()
    to_right.wait_recv()
    edge_y = [jnp.zeros((2 * halves, 128), jnp.float32)] * 2
    edge_flux = list(edge_y)
    for k in range(levels):
        inv_k = inv[k, pl.ds(0, 2 * halves), :]
        for e in range(2):
            edge_part[e, k] = edge_y[e]
            edge_flux[e] = edge_flux[e] + (edge_y[e] - NEW_WEIGHT * edge_in[e, k])
            edge_y[e] = edge_y[e] + edge_flux[e] * inv_k
    for e in range(2):
        for q in range(2):
            for h in range(halves):
                tile, row, c = h + e * (n - halves), 7 * e, q * halves + h
                for i, value in enumerate((edge_y[e], edge_flux[e])):
                    at = ends.at[tile, 2 * q + i, pl.ds(row, 1), :]
                    at[...] = at[...] + value[c : c + 1]
    send(False)
    gathered[me] = ends[lax.rem(me * back_stride, n)]

    @pl.when(me < n - 1)
    def _():
        for c in up_copies:
            c.start()

    @pl.when(me > 0)
    def _():
        for c in down_copies:
            c.start()

    def edge_rows(k, carry):
        for e in range(2):
            row = e * (rows - 1)
            for q, (tend, part) in enumerate(((tend_t, part_t), (tend_w, part_w))):
                for h in range(halves):
                    c = q * halves + h
                    at = (k, pl.ds(row, 1), pl.ds(h * 128, 128))
                    tend[at] = tend[at] + edge_in[e, k, pl.ds(c, 1), :]
                    part[at] = part[at] + edge_part[e, k, pl.ds(c, 1), :]
        return carry

    lax.fori_loop(0, levels, edge_rows, 0)

    for step in range(2, n - 1):
        mat_copy(lax.rem(me + step, n), me).wait_recv()

    def entry_of(d, r):
        return jnp.broadcast_to(mats[d, pl.ds(r, 1), :], (8, 128))

    bottom = [(one, entry_of(0, 4))]
    for d in range(n):
        a, b = bottom[-1]
        bottom.append(
            (entry_of(d, 0) * a + entry_of(d, 1) * b, entry_of(d, 2) * a + entry_of(d, 3) * b)
        )
    top = [(zero, one)]
    for d in range(n - 1, -1, -1):
        a, b = top[-1]
        top.append(
            (entry_of(d, 3) * a + entry_of(d, 1) * b, entry_of(d, 2) * a + entry_of(d, 0) * b)
        )
    top = top[::-1]
    scale = 1.0 / bottom[n][0]

    for step in range(1, n):
        fwd_copy(0, lax.rem(me + step, n), me).wait_recv()

    for q in range(2):
        amp = [None] * n
        run = zero
        for d in range(n - 1, -1, -1):
            a, b = top[d + 1]
            run = run - (gathered[d, 2 * q] * b + gathered[d, 2 * q + 1] * a)
            amp[d] = run * scale
        run = zero
        for d in range(n):
            bot, up = bottom[d], top[d]
            beta = run * scale
            sols[d, 2 * q] = bot[0] * amp[d] - up[0] * beta
            sols[d, 2 * q + 1] = bot[1] * amp[d] + up[1] * beta
            a, b = bottom[d + 1]
            run = run + (a * gathered[d, 2 * q + 1] - b * gathered[d, 2 * q])

    def back_copy(src, dst):
        return pltpu.make_async_remote_copy(
            src_ref=sols.at[dst],
            dst_ref=entry.at[src],
            send_sem=back_send.at[dst],
            recv_sem=back_recv.at[src],
            device_id={"gz": dst},
            device_id_type=MESH,
        )

    for mask in far_first(n):
        back_copy(me, jnp.bitwise_xor(me, mask)).start()
    entry[me] = sols[me]
    @pl.when(me > 0)
    def _():
        for c in up_copies:
            c.wait_recv()

    @pl.when(me < n - 1)
    def _():
        for c in down_copies:
            c.wait_recv()

    for q, tend in enumerate((tend_t, tend_w)):
        tend[0] = tend[0] + met_s[0] * (below[1] * below[q])
        tend[levels - 1] = tend[levels - 1] - met_s[levels - 1] * (above[1] * above[q])

    for step in range(1, n):
        back_copy(lax.rem(me + step, n), me).wait_recv()
    for tile in range(n):
        ib, h = tile // halves, tile % halves
        r, c = 8 * ib, 128 * h
        own = (tile * stride) % n
        for q, buf in enumerate((tbuf, wbuf)):
            lo = m_below * (wbuf[0, h, pl.ds(r + PAD, 8), :] * buf[0, h, pl.ds(r + PAD, 8), :])
            state[2 * q, pl.ds(r, 8), pl.ds(c, 128)] = entry[own, 2 * q] + inv_low * lo
            state[2 * q + 1, pl.ds(r, 8), pl.ds(c, 128)] = entry[own, 2 * q + 1] + lo

    @pl.when(me < n - 1)
    def _():
        for c in up_copies:
            c.wait_send()

    @pl.when(me > 0)
    def _():
        for c in down_copies:
            c.wait_send()

    to_left.wait_send()
    to_right.wait_send()
    for step in range(1, n):
        mat_copy(me, lax.rem(me + step, n)).wait_send()
        fwd_copy(0, me, lax.rem(me + step, n)).wait_send()
        back_copy(me, lax.rem(me + step, n)).wait_send()


def finish_kernel(
    part_t, part_w, tend_t, tend_w, state, basis,
    temp_next, w_next, tend_t_out, tend_w_out,
    xbuf, sems,
):
    levels, rows, cols = part_t.shape
    outs = [
        pltpu.make_async_copy(tend_t, tend_t_out, sems.at[0]),
        pltpu.make_async_copy(tend_w, tend_w_out, sems.at[1]),
    ]
    for c in outs:
        c.start()

    def level(k):
        phi = jnp.concatenate([basis[0, k]] * (cols // 128), axis=1)[:1]
        psi = jnp.concatenate([basis[1, k]] * (cols // 128), axis=1)[:1]
        for q, part in enumerate((part_t, part_w)):
            xbuf[q, k] = part[k] + phi * state[2 * q] + psi * state[2 * q + 1]

    for k in range(levels):
        level(k)
        for q, out in enumerate((temp_next, w_next)):
            c = pltpu.make_async_copy(xbuf.at[q, k], out.at[k], sems.at[2 + q * levels + k])
            c.start()
            outs.append(c)
    for c in outs:
        c.wait()


def local(n, temp, u_vel, v_vel, w_vel, temp_old, w_old, lower, upper, metric):
    levels, rows, cols = temp.shape
    halves = cols // 128
    f32 = jnp.float32
    cube = jax.ShapeDtypeStruct((levels, rows, cols), f32)
    hbm = pl.BlockSpec(memory_space=pltpu.HBM)
    vmem = pl.BlockSpec(memory_space=pltpu.VMEM)
    dma = pltpu.SemaphoreType.DMA
    padded = pltpu.VMEM((levels, halves, rows + 2 * PAD, 128), f32)
    plain = pltpu.VMEM((levels, halves, rows, 128), f32)
    edge = pltpu.VMEM((2, levels, 2 * halves, 128), f32)
    parts = pl.pallas_call(
        functools.partial(exchange_kernel, n),
        out_shape=(
            cube, cube, cube, cube,
            jax.ShapeDtypeStruct((4, rows, cols), f32),
            jax.ShapeDtypeStruct((2, levels, 8, 128), f32),
        ),
        in_specs=[hbm] * 9,
        out_specs=(vmem,) * 6,
        scratch_shapes=[
            padded, padded, padded, plain, plain, plain,
            pltpu.SMEM((levels,), f32), pltpu.SMEM((levels,), f32), pltpu.SMEM((levels,), f32),
            pltpu.VMEM((levels, 8, 128), f32),
            pltpu.VMEM((4, 8, 128), f32),
            pltpu.VMEM((n, 8, 128), f32),
            edge, edge, edge,
            pltpu.VMEM((2, rows, cols), f32),
            pltpu.VMEM((2, rows, cols), f32),
            pltpu.VMEM((n, 4, 8, 128), f32),
            pltpu.VMEM((n, 4, 8, 128), f32),
            pltpu.VMEM((n, 4, 8, 128), f32),
            pltpu.VMEM((n, 4, 8, 128), f32),
            dma((6, halves)), dma((3,)),
            dma((n,)), dma((n,)), dma((2,)), dma((2,)), dma((2, 2)), dma((2, 2)),
            dma((n,)), dma((n,)), dma((n,)), dma((n,)),
        ],
        compiler_params=pltpu.CompilerParams(
            collective_id=0, has_side_effects=True, vmem_limit_bytes=40 * 1024 * 1024
        ),
        name="exchange",
    )(
        *(
            pltpu.with_memory_space_constraint(x, pltpu.HBM)
            for x in (temp, u_vel, v_vel, w_vel, temp_old, w_old, lower, upper, metric)
        )
    )
    return pl.pallas_call(
        finish_kernel,
        out_shape=(cube,) * 4,
        in_specs=[vmem] * 6,
        out_specs=(hbm,) * 4,
        scratch_shapes=[pltpu.VMEM((2, levels, rows, cols), f32), dma((2 + 2 * levels,))],
        compiler_params=pltpu.CompilerParams(vmem_limit_bytes=24 * 1024 * 1024),
        name="finish",
    )(*parts)


def solution(mesh):
    cube = P("gz", "gx", None)
    line = P("gz")
    return jax.shard_map(
        functools.partial(local, mesh.shape["gz"]),
        mesh=mesh,
        in_specs=(cube,) * 6 + (line,) * 3,
        out_specs=(cube,) * 4,
        check_vma=False,
    )
```

```python
import functools

import jax
import jax.numpy as jnp
from jax import lax
from jax.experimental import pallas as pl
from jax.experimental.pallas import tpu as pltpu
from jax.sharding import PartitionSpec as P

NEW_WEIGHT = 5.0 / 12.0
OLD_WEIGHT = -17.0 / 60.0
HORIZ_DIFF = 0.1
MESH = pl.DeviceIdType.MESH
PAD = 8


def hops(mask):
    along_x = (0, 1, 2, 1)[(mask >> 1) & 3]
    return 4 * (along_x + 2 * (mask >> 3)) + (mask & 1)


def far_first(n):
    return sorted(range(1, n), key=hops, reverse=True)


def exchange_kernel(
    n, temp, u_vel, v_vel, w_vel, temp_old, w_old, lower, upper, metric,
    part_t, part_w, tend_t, tend_w, state, basis,
    tbuf, ubuf, wbuf, vbuf, tobuf, wobuf,
    low_s, up_s, met_s,
    inv, mine, near, edge_out, edge_in, edge_part, below, above,
    ends, gathered, sols, entry,
    load_sem, scal_sem, near_send, near_recv, edge_send, edge_recv, wall_send, wall_recv,
    fwd_send, fwd_recv, back_send, back_recv,
):
    levels, rows, cols = temp.shape
    halves = cols // 128
    blocks = rows // 8
    me = lax.axis_index("gz")
    gx = lax.axis_index("gx")
    nx = lax.axis_size("gx")
    right = lax.rem(gx + 1, nx)
    left = lax.rem(gx + nx - 1, nx)

    scal = [
        pltpu.make_async_copy(src, dst, scal_sem.at[i])
        for i, (src, dst) in enumerate(((lower, low_s), (upper, up_s), (metric, met_s)))
    ]
    for c in scal:
        c.start()
    loads = []
    for i, (src, dst) in enumerate(
        ((temp, tbuf), (w_vel, wbuf), (u_vel, ubuf), (v_vel, vbuf), (temp_old, tobuf), (w_old, wobuf))
    ):
        first = PAD if i < 3 else 0
        for h in range(halves):
            c = pltpu.make_async_copy(
                src.at[:, :, pl.ds(h * 128, 128)],
                dst.at[:, h, pl.ds(first, rows), :],
                load_sem.at[i, h],
            )
            c.start()
            loads.append(c)

    def clear(k, carry):
        for buf in (tbuf, wbuf, ubuf):
            for h in range(halves):
                buf[k, h, pl.ds(0, PAD), :] = jnp.zeros((PAD, 128), jnp.float32)
                buf[k, h, pl.ds(rows + PAD, PAD), :] = jnp.zeros((PAD, 128), jnp.float32)
        return carry

    barrier = pltpu.get_barrier_semaphore()
    for other in (left, right):
        pl.semaphore_signal(barrier, inc=1, device_id={"gx": other}, device_id_type=MESH)
    for mask in far_first(n):
        pl.semaphore_signal(
            barrier, inc=1, device_id={"gz": jnp.bitwise_xor(me, mask)}, device_id_type=MESH
        )

    lax.fori_loop(0, levels, clear, 0)
    for c in loads[: 3 * halves]:
        c.wait()

    def pack(k, carry):
        for e, (row, sign) in enumerate(((PAD, -0.5), (PAD + rows - 1, 0.5))):
            for h in range(halves):
                weight = HORIZ_DIFF + sign * ubuf[k, h, pl.ds(row, 1), :]
                for q, buf in enumerate((tbuf, wbuf)):
                    edge_out[e, k, pl.ds(q * halves + h, 1), :] = weight * buf[k, h, pl.ds(row, 1), :]
        return carry

    lax.fori_loop(0, levels, pack, 0)

    for c in scal:
        c.wait()
    one = jnp.ones((8, 128), jnp.float32)
    zero = jnp.zeros((8, 128), jnp.float32)
    phi, phi_flux, psi, psi_flux = one, zero, zero, one
    for k in range(levels):
        inv_k = 1.0 / (one * up_s[k])
        inv[k] = inv_k
        basis[0, k] = phi
        basis[1, k] = psi
        phi_flux = phi_flux + phi
        psi_flux = psi_flux + psi
        phi = phi + phi_flux * inv_k
        psi = psi + psi_flux * inv_k
    sub = lax.broadcasted_iota(jnp.int32, (8, 128), 0)
    mine[0] = phi
    mine[1] = psi
    mine[2] = phi_flux
    mine[3] = psi_flux
    mat = jnp.where(sub == 0, phi, zero)
    mat = jnp.where(sub == 1, psi, mat)
    mat = jnp.where(sub == 2, phi_flux, mat)
    mat = jnp.where(sub == 3, psi_flux, mat)
    mat = jnp.where(sub == 4, one * low_s[0], mat)
    mat = jnp.where(sub == 5, one * met_s[0], mat)
    mat = jnp.where(sub == 6, one * met_s[levels - 1], mat)
    near[0] = mat
    for tile in range(n):
        ends[tile, 4] = mat

    pl.semaphore_wait(barrier, n + 1)

    above_id = lax.rem(me + 1, n)
    below_id = lax.rem(me + n - 1, n)
    near_copies = [
        pltpu.make_async_remote_copy(
            src_ref=near.at[0],
            dst_ref=near.at[2 - i],
            send_sem=near_send.at[i],
            recv_sem=near_recv.at[1 - i],
            device_id={"gz": other},
            device_id_type=MESH,
        )
        for i, other in enumerate((above_id, below_id))
    ]
    for c in near_copies:
        c.start()

    to_left = pltpu.make_async_remote_copy(
        src_ref=edge_out.at[0], dst_ref=edge_in.at[1], send_sem=edge_send.at[0], recv_sem=edge_recv.at[0],
        device_id={"gx": left}, device_id_type=MESH,
    )
    to_right = pltpu.make_async_remote_copy(
        src_ref=edge_out.at[1], dst_ref=edge_in.at[0], send_sem=edge_send.at[1], recv_sem=edge_recv.at[1],
        device_id={"gx": right}, device_id_type=MESH,
    )
    to_left.start()
    to_right.start()

    up_copies = [
        pltpu.make_async_remote_copy(
            src_ref=src.at[levels - 1],
            dst_ref=below.at[i],
            send_sem=wall_send.at[0, i],
            recv_sem=wall_recv.at[0, i],
            device_id={"gz": lax.rem(me + 1, n)},
            device_id_type=MESH,
        )
        for i, src in enumerate((temp, w_vel))
    ]
    down_copies = [
        pltpu.make_async_remote_copy(
            src_ref=src.at[0],
            dst_ref=above.at[i],
            send_sem=wall_send.at[1, i],
            recv_sem=wall_recv.at[1, i],
            device_id={"gz": lax.rem(me + n - 1, n)},
            device_id_type=MESH,
        )
        for i, src in enumerate((temp, w_vel))
    ]

    @pl.when(me == 0)
    def _():
        below[...] = jnp.zeros_like(below)

    @pl.when(me == n - 1)
    def _():
        above[...] = jnp.zeros_like(above)

    for c in loads[3 * halves :]:
        c.wait()

    lane = lax.broadcasted_iota(jnp.int32, (8, 128), 1)
    first_lane = lane == 0
    last_lane = lane == 127

    def next_col(g):
        r = [pltpu.roll(x, 127, 1) for x in g]
        return [jnp.where(last_lane, r[(h + 1) % halves], r[h]) for h in range(halves)]

    def prev_col(g):
        r = [pltpu.roll(x, 1, 1) for x in g]
        return [jnp.where(first_lane, r[(h - 1) % halves], r[h]) for h in range(halves)]

    def block(ib):
        row = pl.multiple_of(ib * 8, 8)
        H = range(halves)

        def center(buf, k):
            return [buf[k, h, pl.ds(row + PAD, 8), :] for h in H]

        y = [[zero for _ in H] for _ in range(2)]
        flux = [[zero for _ in H] for _ in range(2)]
        f = [center(tbuf, 0), center(wbuf, 0)]
        wf = [[f[1][h] * f[q][h] for h in H] for q in range(2)]
        wf_below = [[zero for _ in H] for _ in range(2)]
        for k in range(levels):
            if k < levels - 1:
                f_up = [center(tbuf, k + 1), center(wbuf, k + 1)]
                wf_up = [[f_up[1][h] * f_up[q][h] for h in H] for q in range(2)]
            else:
                f_up, wf_up = None, [[zero for _ in H] for _ in range(2)]
            m_k = met_s[k]
            inv_k = inv[k]
            from_hi, from_lo, y_hi, y_lo = [], [], [], []
            for h in H:
                from_hi.append(HORIZ_DIFF - 0.5 * ubuf[k, h, pl.ds(row + PAD + 1, 8), :])
                from_lo.append(HORIZ_DIFF + 0.5 * ubuf[k, h, pl.ds(row + PAD - 1, 8), :])
                hv = 0.5 * vbuf[k, h, pl.ds(row, 8), :]
                y_hi.append(HORIZ_DIFF - hv)
                y_lo.append(HORIZ_DIFF + hv)
            for q, (buf, old, tend, part) in enumerate(
                ((tbuf, tobuf, tend_t, part_t), (wbuf, wobuf, tend_w, part_w))
            ):
                nxt = next_col([f[q][h] * y_hi[h] for h in H])
                prv = prev_col([f[q][h] * y_lo[h] for h in H])
                for h in H:
                    acc = (
                        buf[k, h, pl.ds(row + PAD + 1, 8), :] * from_hi[h]
                        + buf[k, h, pl.ds(row + PAD - 1, 8), :] * from_lo[h]
                    )
                    acc = acc + (nxt[h] + prv[h])
                    acc = acc + (f[1 - q][h] - (4.0 * HORIZ_DIFF) * f[q][h])
                    acc = acc + m_k * (wf_below[q][h] - wf_up[q][h])
                    tend[k, pl.ds(row, 8), pl.ds(h * 128, 128)] = acc
                    rhs = (
                        (f[q][h] + f[q][h])
                        + NEW_WEIGHT * acc
                        + OLD_WEIGHT * old[k, h, pl.ds(row, 8), :]
                    )
                    part[k, pl.ds(row, 8), pl.ds(h * 128, 128)] = y[q][h] - f[q][h]
                    flux[q][h] = flux[q][h] + (y[q][h] - rhs)
                    y[q][h] = y[q][h] + flux[q][h] * inv_k
            wf_below, wf, f = wf, wf_up, f_up
        for h in H:
            for q in range(2):
                ends[ib * halves + h, 2 * q] = y[q][h]
                ends[ib * halves + h, 2 * q + 1] = flux[q][h]

    def fwd_copy(tile, src, dst):
        return pltpu.make_async_remote_copy(
            src_ref=ends.at[tile],
            dst_ref=gathered.at[src],
            send_sem=fwd_send.at[dst],
            recv_sem=fwd_recv.at[src],
            device_id={"gz": dst},
            device_id_type=MESH,
        )

    stride = 5

    back_stride = pow(stride, -1, n)

    def fix(tile):
        ib = tile // halves
        h = lax.rem(tile, halves)
        r = pl.multiple_of(ib * 8 + PAD, 8)
        for q, buf in enumerate((tbuf, wbuf)):
            lo = m_below * (wbuf[0, h, pl.ds(r, 8), :] * buf[0, h, pl.ds(r, 8), :])
            hi = m_above * (wbuf[levels - 1, h, pl.ds(r, 8), :] * buf[levels - 1, h, pl.ds(r, 8), :])
            ends[tile, 2 * q] = ends[tile, 2 * q] + low_value * lo
            ends[tile, 2 * q + 1] = ends[tile, 2 * q + 1] + low_flux * lo - hi

    def send(inner_tiles):
        for mask in far_first(n):
            dst = jnp.bitwise_xor(me, mask)
            tile = lax.rem(dst * back_stride, n)
            inside = jnp.logical_and(tile >= halves, tile < n - halves)

            @pl.when(inside if inner_tiles else jnp.logical_not(inside))
            def _():
                fwd_copy(tile, me, dst).start()

    inner = blocks - 2

    def block_step(ib, carry):
        block(ib)
        return carry

    lax.fori_loop(0, blocks, block_step, 0)

    for c in near_copies:
        c.wait_recv()
    m_above = jnp.where(me < n - 1, NEW_WEIGHT, 0.0) * jnp.broadcast_to(
        near[1, pl.ds(5, 1), :], (8, 128)
    )
    m_below = jnp.where(me > 0, NEW_WEIGHT, 0.0) * jnp.broadcast_to(
        near[2, pl.ds(6, 1), :], (8, 128)
    )
    inv_low = 1.0 / (one * low_s[0])
    low_value = mine[0] * inv_low + mine[1]
    low_flux = mine[2] * inv_low + mine[3]

    def fix_step(tile, carry):
        fix(tile)
        return carry

    lax.fori_loop(0, n, fix_step, 0)
    send(True)

    to_left.wait_recv()
    to_right.wait_recv()
    edge_y = [jnp.zeros((2 * halves, 128), jnp.float32)] * 2
    edge_flux = list(edge_y)
    for k in range(levels):
        inv_k = inv[k, pl.ds(0, 2 * halves), :]
        for e in range(2):
            edge_part[e, k] = edge_y[e]
            edge_flux[e] = edge_flux[e] + (edge_y[e] - NEW_WEIGHT * edge_in[e, k])
            edge_y[e] = edge_y[e] + edge_flux[e] * inv_k
    for e in range(2):
        for q in range(2):
            for h in range(halves):
                tile, row, c = h + e * (n - halves), 7 * e, q * halves + h
                for i, value in enumerate((edge_y[e], edge_flux[e])):
                    at = ends.at[tile, 2 * q + i, pl.ds(row, 1), :]
                    at[...] = at[...] + value[c : c + 1]
    send(False)
    gathered[me] = ends[lax.rem(me * back_stride, n)]

    @pl.when(me < n - 1)
    def _():
        for c in up_copies:
            c.start()

    @pl.when(me > 0)
    def _():
        for c in down_copies:
            c.start()

    def edge_rows(k, carry):
        for e in range(2):
            row = e * (rows - 1)
            for q, (tend, part) in enumerate(((tend_t, part_t), (tend_w, part_w))):
                for h in range(halves):
                    c = q * halves + h
                    at = (k, pl.ds(row, 1), pl.ds(h * 128, 128))
                    tend[at] = tend[at] + edge_in[e, k, pl.ds(c, 1), :]
                    part[at] = part[at] + edge_part[e, k, pl.ds(c, 1), :]
        return carry

    lax.fori_loop(0, levels, edge_rows, 0)

    for step in range(1, n):
        fwd_copy(0, lax.rem(me + step, n), me).wait_recv()

    def entry_of(d, r):
        return jnp.broadcast_to(gathered[d, 4, pl.ds(r, 1), :], (8, 128))

    bottom = [(one, entry_of(0, 4))]
    for d in range(n):
        a, b = bottom[-1]
        bottom.append(
            (entry_of(d, 0) * a + entry_of(d, 1) * b, entry_of(d, 2) * a + entry_of(d, 3) * b)
        )
    top = [(zero, one)]
    for d in range(n - 1, -1, -1):
        a, b = top[-1]
        top.append(
            (entry_of(d, 3) * a + entry_of(d, 1) * b, entry_of(d, 2) * a + entry_of(d, 0) * b)
        )
    top = top[::-1]
    scale = 1.0 / bottom[n][0]

    for q in range(2):
        amp = [None] * n
        run = zero
        for d in range(n - 1, -1, -1):
            a, b = top[d + 1]
            run = run - (gathered[d, 2 * q] * b + gathered[d, 2 * q + 1] * a)
            amp[d] = run * scale
        run = zero
        for d in range(n):
            bot, up = bottom[d], top[d]
            beta = run * scale
            sols[d, 2 * q] = bot[0] * amp[d] - up[0] * beta
            sols[d, 2 * q + 1] = bot[1] * amp[d] + up[1] * beta
            a, b = bottom[d + 1]
            run = run + (a * gathered[d, 2 * q + 1] - b * gathered[d, 2 * q])

    def back_copy(src, dst):
        return pltpu.make_async_remote_copy(
            src_ref=sols.at[dst],
            dst_ref=entry.at[src],
            send_sem=back_send.at[dst],
            recv_sem=back_recv.at[src],
            device_id={"gz": dst},
            device_id_type=MESH,
        )

    for mask in far_first(n):
        back_copy(me, jnp.bitwise_xor(me, mask)).start()
    entry[me] = sols[me]
    @pl.when(me > 0)
    def _():
        for c in up_copies:
            c.wait_recv()

    @pl.when(me < n - 1)
    def _():
        for c in down_copies:
            c.wait_recv()

    for q, tend in enumerate((tend_t, tend_w)):
        tend[0] = tend[0] + met_s[0] * (below[1] * below[q])
        tend[levels - 1] = tend[levels - 1] - met_s[levels - 1] * (above[1] * above[q])

    for step in range(1, n):
        back_copy(lax.rem(me + step, n), me).wait_recv()
    for tile in range(n):
        ib, h = tile // halves, tile % halves
        r, c = 8 * ib, 128 * h
        own = (tile * stride) % n
        for q, buf in enumerate((tbuf, wbuf)):
            lo = m_below * (wbuf[0, h, pl.ds(r + PAD, 8), :] * buf[0, h, pl.ds(r + PAD, 8), :])
            state[2 * q, pl.ds(r, 8), pl.ds(c, 128)] = entry[own, 2 * q] + inv_low * lo
            state[2 * q + 1, pl.ds(r, 8), pl.ds(c, 128)] = entry[own, 2 * q + 1] + lo

    @pl.when(me < n - 1)
    def _():
        for c in up_copies:
            c.wait_send()

    @pl.when(me > 0)
    def _():
        for c in down_copies:
            c.wait_send()

    for c in (to_left, to_right, *near_copies):
        c.wait_send()
    for step in range(1, n):
        fwd_copy(0, me, lax.rem(me + step, n)).wait_send()
        back_copy(me, lax.rem(me + step, n)).wait_send()


def finish_kernel(
    part_t, part_w, tend_t, tend_w, state, basis,
    temp_next, w_next, tend_t_out, tend_w_out,
    xbuf, sems,
):
    levels, rows, cols = part_t.shape
    outs = [
        pltpu.make_async_copy(tend_t, tend_t_out, sems.at[0]),
        pltpu.make_async_copy(tend_w, tend_w_out, sems.at[1]),
    ]
    for c in outs:
        c.start()

    def level(k):
        phi = jnp.concatenate([basis[0, k]] * (cols // 128), axis=1)[:1]
        psi = jnp.concatenate([basis[1, k]] * (cols // 128), axis=1)[:1]
        for q, part in enumerate((part_t, part_w)):
            xbuf[q, k] = part[k] + phi * state[2 * q] + psi * state[2 * q + 1]

    for k in range(levels):
        level(k)
        for q, out in enumerate((temp_next, w_next)):
            c = pltpu.make_async_copy(xbuf.at[q, k], out.at[k], sems.at[2 + q * levels + k])
            c.start()
            outs.append(c)
    for c in outs:
        c.wait()


def local(n, temp, u_vel, v_vel, w_vel, temp_old, w_old, lower, upper, metric):
    levels, rows, cols = temp.shape
    halves = cols // 128
    f32 = jnp.float32
    cube = jax.ShapeDtypeStruct((levels, rows, cols), f32)
    hbm = pl.BlockSpec(memory_space=pltpu.HBM)
    vmem = pl.BlockSpec(memory_space=pltpu.VMEM)
    dma = pltpu.SemaphoreType.DMA
    padded = pltpu.VMEM((levels, halves, rows + 2 * PAD, 128), f32)
    plain = pltpu.VMEM((levels, halves, rows, 128), f32)
    edge = pltpu.VMEM((2, levels, 2 * halves, 128), f32)
    parts = pl.pallas_call(
        functools.partial(exchange_kernel, n),
        out_shape=(
            cube, cube, cube, cube,
            jax.ShapeDtypeStruct((4, rows, cols), f32),
            jax.ShapeDtypeStruct((2, levels, 8, 128), f32),
        ),
        in_specs=[hbm] * 9,
        out_specs=(vmem,) * 6,
        scratch_shapes=[
            padded, padded, padded, plain, plain, plain,
            pltpu.SMEM((levels,), f32), pltpu.SMEM((levels,), f32), pltpu.SMEM((levels,), f32),
            pltpu.VMEM((levels, 8, 128), f32),
            pltpu.VMEM((4, 8, 128), f32),
            pltpu.VMEM((3, 8, 128), f32),
            edge, edge, edge,
            pltpu.VMEM((2, rows, cols), f32),
            pltpu.VMEM((2, rows, cols), f32),
            pltpu.VMEM((n, 5, 8, 128), f32),
            pltpu.VMEM((n, 5, 8, 128), f32),
            pltpu.VMEM((n, 4, 8, 128), f32),
            pltpu.VMEM((n, 4, 8, 128), f32),
            dma((6, halves)), dma((3,)),
            dma((2,)), dma((2,)), dma((2,)), dma((2,)), dma((2, 2)), dma((2, 2)),
            dma((n,)), dma((n,)), dma((n,)), dma((n,)),
        ],
        compiler_params=pltpu.CompilerParams(
            collective_id=0, has_side_effects=True, vmem_limit_bytes=40 * 1024 * 1024
        ),
        name="exchange",
    )(
        *(
            pltpu.with_memory_space_constraint(x, pltpu.HBM)
            for x in (temp, u_vel, v_vel, w_vel, temp_old, w_old, lower, upper, metric)
        )
    )
    return pl.pallas_call(
        finish_kernel,
        out_shape=(cube,) * 4,
        in_specs=[vmem] * 6,
        out_specs=(hbm,) * 4,
        scratch_shapes=[pltpu.VMEM((2, levels, rows, cols), f32), dma((2 + 2 * levels,))],
        compiler_params=pltpu.CompilerParams(vmem_limit_bytes=24 * 1024 * 1024),
        name="finish",
    )(*parts)


def solution(mesh):
    cube = P("gz", "gx", None)
    line = P("gz")
    return jax.shard_map(
        functools.partial(local, mesh.shape["gz"]),
        mesh=mesh,
        in_specs=(cube,) * 6 + (line,) * 3,
        out_specs=(cube,) * 4,
        check_vma=False,
    )
```
